32 devices in a mesh: wide: 8 (over y, x, core), narrow: 4 (over z).
Axes of the slice: x: 2, y: 2, z: 4, core: 2. Of those that a mesh axis runs over, the one named last changes fastest.
Arguments:
- residual: bfloat16 [192, 16384], P(('wide', 'narrow')), may hold values from -10 to 10
- queries: bfloat16 [192, 16384], P(('wide', 'narrow')), may hold values from -10 to 10
- keys: bfloat16 [192, 8, 256, 128], P(('wide', 'narrow')), may hold values from -6 to 6
- values: bfloat16 [192, 8, 256, 128], P(('wide', 'narrow')), may hold values from -6 to 6
- cache_lengths: int32 [192], P(('wide', 'narrow')), may hold values from 2 to 256, as said below
- track_numbers: int32 [192], P(('wide', 'narrow')), may hold values from 0 to 15
- track_table: bfloat16 [16, 16384], replicated, may hold values from -3 to 3
- norm_gain: bfloat16 [16384], replicated, may hold values from 0.099609375 to 1.8984375
- gate_weight: bfloat16 [16384, 28672], P('narrow', 'wide'), may hold values from -0.046875 to 0.046875
- up_weight: bfloat16 [16384, 28672], P('narrow', 'wide'), may hold values from -0.046875 to 0.046875
- down_weight: bfloat16 [28672, 16384], P('wide', 'narrow'), may hold values from -0.046875 to 0.046875
Outputs:
- attended: bfloat16 [192, 16384], P(('wide', 'narrow'))
- ffn_out: bfloat16 [192, 16384], P(('wide', 'narrow'))
The draws below stay inside these ranges and needn't reach their ends.
Inputs may be any that keep to these rules, and one draw needn't show every extreme that they name: `cache_lengths`: positions below a sequence's length hold its keys and values; some sequence fills all 256 positions.
All inputs are finite; a program needn't handle non-finite values.
Results may differ from the reference program's by a relative error of at most 0.0067.
Values may be sent and summed in bfloat16 or wider, within the bound.
A program may use at most 192 MiB of HBM per device.

```python
import math
import jax
import jax.numpy as jnp
from jax import lax

D = 16384
QHEADS = 128
KVHEADS = 8
HDIM = 128
FF = 28672
TRACKS = 16
LCACHE = 256
GROUP = 16
BATCH = 192


def drawn_pair(key):
    base = jax.random.fold_in(key, 11)
    key_query, key_key = jax.random.split(base, 2)
    query_shape = (BATCH, KVHEADS, GROUP, HDIM)
    key_shape = (BATCH, KVHEADS, LCACHE, HDIM)
    query_draw = jnp.clip(1.5 * jax.random.normal(key_query, query_shape, jnp.float32), -6.0, 6.0)
    key_draw = jnp.clip(1.3 * jax.random.normal(key_key, key_shape, jnp.float32), -6.0, 6.0)
    return (query_draw.reshape(BATCH, QHEADS * HDIM), key_draw)


def draw_queries(key, part):
    return drawn_pair(key)[0].astype(jnp.bfloat16)


def draw_keys(key, part):
    return drawn_pair(key)[1].astype(jnp.bfloat16)


def draw_residual(key, part):
    key_noise, key_column = jax.random.split(jax.random.fold_in(key, 23), 2)
    column = jnp.power(10.0, jax.random.uniform(key_column, (D,), jnp.float32, -0.5, 0.5))
    noise = jnp.clip(jax.random.normal(key_noise, (BATCH, D), jnp.float32), -6.0, 6.0)
    result = 0.5 * column * noise
    return jnp.clip(result, -10.0, 10.0).astype(jnp.bfloat16)


def draw_cache_lengths(key, part):
    lengths = jax.random.randint(jax.random.fold_in(key, 31), (BATCH,), 2, LCACHE + 1)
    lengths = lengths.at[0].set(LCACHE)
    lengths = lengths.at[1].set(2)
    return lengths.astype(jnp.int32)


def place_ends(array, stream_key, smallest, largest):
    place = [jax.random.randint(jax.random.fold_in(stream_key, axis), (), 0, length) for axis, length in enumerate(array.shape)]
    longest = array.shape.index(max(array.shape))
    next_to = place[:longest] + [(place[longest] + 1) % array.shape[longest]] + place[longest + 1:]
    return array.at[tuple(place)].set(smallest).at[tuple(next_to)].set(largest)


def spiked(values, rng, source, target, blocks, factor):
    def block_of(dim):
        return (jnp.arange(values.shape[dim]) // (values.shape[dim] // blocks)).reshape((-1,) + (1,) * (values.ndim - 1 - dim))

    near = jax.random.permutation(rng, blocks)[block_of(target)]
    second = (block_of(target) + blocks // 2) % blocks
    return jnp.where((block_of(source) == near) | (block_of(source) == second), factor * values, values)


def levels(own_key, dims, cuts, smallest, top_value):
    factor_of, own = 1.0, jax.random.fold_in(own_key, 6)
    for axis_at, parts in cuts:
        draws = jnp.exp(jax.random.uniform(jax.random.fold_in(own, axis_at), (parts,), jnp.float32, smallest / len(cuts), top_value / len(cuts)))
        factor_of = factor_of * jnp.repeat(draws, dims[axis_at] // parts).reshape([-1 if axis == axis_at else 1 for axis in range(len(dims))])
    return factor_of


def bell_draw(rng, extent, spread, bound, cuts=(), kind=jnp.bfloat16):
    entries = jax.random.normal(rng, extent, jnp.float32) * spread
    if len(cuts) > 0:
        entries = levels(rng, extent, cuts, -0.22, 0.18) * entries
    return jnp.clip(entries, min=-bound, max=bound).astype(kind)


def noise_with(rng, extent, spread, bound, cuts, heavy, kind=jnp.bfloat16):
    values = spread * jax.random.normal(rng, extent, jnp.float32)
    if cuts:
        values = values * levels(rng, extent, cuts, -0.22, 0.18)
    return jnp.clip(spiked(values, jax.random.fold_in(rng, 3), *heavy), -bound, bound).astype(kind)


def setup_inputs(seed: int = 0) -> dict:
    arg_keys = jax.random.split(jax.random.key(seed), 12)
    return {
        "residual": draw_residual(jax.random.fold_in(arg_keys[11], 71), 0),
        "queries": draw_queries(jax.random.fold_in(arg_keys[11], 71), 0),
        "keys": draw_keys(jax.random.fold_in(arg_keys[11], 71), 0),
        "values": bell_draw(arg_keys[3], (BATCH, KVHEADS, LCACHE, HDIM), 1.0, 6.0, ((0, 32),)),
        "cache_lengths": draw_cache_lengths(jax.random.fold_in(arg_keys[11], 71), 0),
        "track_numbers": place_ends(jax.random.randint(arg_keys[5], (BATCH,), 0, TRACKS), jax.random.fold_in(arg_keys[5], 1), 0, TRACKS - 1).astype(jnp.int32),
        "track_table": bell_draw(arg_keys[6], (TRACKS, D), 0.5, 3.0),
        "norm_gain": jnp.clip(1.0 + 0.18 * jax.random.normal(arg_keys[7], (D,), jnp.float32), 0.099609375, 1.8984375).astype(jnp.bfloat16),
        "gate_weight": bell_draw(arg_keys[8], (D, FF), D ** -0.5, 0.046875, ((0, 4), (1, 8))),
        "up_weight": bell_draw(arg_keys[9], (D, FF), D ** -0.5, 0.046875, ((0, 4), (1, 8))),
        "down_weight": noise_with(arg_keys[10], (FF, D), FF ** -0.5, 0.046875, ((0, 8), (1, 4)), (0, 1, 8, 2.0)),
    }


def reference(residual, queries, keys, values, cache_lengths, track_numbers, track_table, norm_gain, gate_weight, up_weight, down_weight):
    grouped = queries.astype(jnp.float32).reshape(BATCH, KVHEADS, GROUP, HDIM)
    scores = jnp.einsum('bkgd,bkld->bkgl', grouped, keys.astype(jnp.float32)) / math.sqrt(HDIM)
    visible = jnp.arange(LCACHE, dtype=jnp.int32)[None, :] < cache_lengths.astype(jnp.int32)[:, None]
    scores = jnp.where(visible[:, None, None, :], scores, -jnp.inf)
    highest = lax.optimization_barrier(jnp.max(scores, axis=-1, keepdims=True))
    weights = jnp.exp(scores - highest)
    probs = (weights / lax.optimization_barrier(jnp.sum(weights, axis=-1, keepdims=True))).astype(jnp.bfloat16)
    context = jnp.einsum('bkgl,bkld->bkgd', probs.astype(jnp.float32), values.astype(jnp.float32)).reshape(BATCH, D)
    stream = residual.astype(jnp.float32) + context + track_table[track_numbers].astype(jnp.float32)
    attended = stream.astype(jnp.bfloat16)
    scale = jax.lax.rsqrt(lax.optimization_barrier(jnp.mean(stream * stream, axis=-1, keepdims=True)) + 1e-05)
    normed = (stream * scale * norm_gain.astype(jnp.float32)).astype(jnp.bfloat16)
    gate = jnp.dot(normed, gate_weight, preferred_element_type=jnp.float32)
    up = jnp.dot(normed, up_weight, preferred_element_type=jnp.float32)
    hidden = (jax.nn.silu(gate) * up).astype(jnp.bfloat16)
    ffn_out = jnp.dot(hidden, down_weight, preferred_element_type=jnp.float32).astype(jnp.bfloat16)
    return (attended, ffn_out)
```

```python
import functools
import math

import jax
import jax.numpy as jnp
from jax import lax
from jax.experimental import pallas as pl
from jax.experimental.pallas import tpu as pltpu
from jax.sharding import PartitionSpec as P

LAG = 2
VMEM_LIMIT = 66_000_000


def flip(index, bit):
    step = 2**bit
    return index + step * (1 - 2 * ((index // step) % 2))


def flips(index, bits):
    found = [index]
    for bit in bits:
        found = found + [flip(one, bit) for one in found]
    return found


def bit_orders(chips):
    count = chips.bit_length() - 1
    bits = list(range(count))
    half = count // 2
    return (bits, bits[half:] + bits[:half])


def meet(peers):
    barrier = pltpu.get_barrier_semaphore()
    for peer in peers:
        pl.semaphore_signal(barrier, inc=1, device_id=peer)
    pl.semaphore_wait(barrier, len(peers))


def gather_kernel(wide, narrow, mine_ref, out_ref, held, own_sem, z_send, z_recv, w_send, w_recv):
    w = lax.axis_index("wide")
    n = lax.axis_index("narrow")
    chips = wide // 2
    orders = bit_orders(chips)
    half = narrow // 2
    steps = wide.bit_length() - 1
    meet(
        [{"narrow": (n + i) % narrow} for i in range(1, narrow)]
        + [{"wide": flip(w, bit)} for bit in range(steps)]
    )

    own = pltpu.make_async_copy(mine_ref.at[n], held.at[w, n], own_sem)
    own.start()
    sends = []
    for i in range(1, narrow):
        to = (n + i) % narrow
        copy = pltpu.make_async_remote_copy(
            src_ref=mine_ref.at[to],
            dst_ref=held.at[w, n],
            send_sem=z_send.at[i],
            recv_sem=z_recv.at[n],
            device_id={"narrow": to},
        )
        copy.start()
        sends.append(copy)
    own.wait()
    for i in range(1, narrow):
        source = (n + i) % narrow
        pltpu.make_async_remote_copy(
            src_ref=mine_ref.at[source],
            dst_ref=held.at[w, source],
            send_sem=z_send.at[i],
            recv_sem=z_recv.at[source],
            device_id={"narrow": source},
        ).wait_recv()

    def block_copy(block, part, number, to):
        return pltpu.make_async_remote_copy(
            src_ref=held.at[block, pl.ds(part * half, half)],
            dst_ref=held.at[block, pl.ds(part * half, half)],
            send_sem=w_send.at[part, number],
            recv_sem=w_recv.at[part, block],
            device_id={"wide": to},
        )

    walks = [[bit + 1 for bit in order] + [0] for order in orders]
    number = 0
    for step in range(steps):
        for part in range(2):
            walk = walks[part]
            to = flip(w, walk[step])
            for k, block in enumerate(flips(w, walk[:step])):
                copy = block_copy(block, part, number + k, to)
                copy.start()
                sends.append(copy)
        for part in range(2):
            walk = walks[part]
            to = flip(w, walk[step])
            for k, block in enumerate(flips(to, walk[:step])):
                block_copy(block, part, number + k, to).wait_recv()
        number += 2**step
    for copy in sends:
        copy.wait_send()
    out_ref[...] = held[...]


def ffn_kernel(
    wide, narrow, chunks, ticks,
    piece_ref, gate_ref, up_ref, down_ref, out_ref,
    mine, arrived, hidden, total, down_held,
    sum_send, sum_recv, hid_send, hid_recv, down_sem,
):
    tick = pl.program_id(0)
    n = lax.axis_index("narrow")
    last = narrow - 1
    rows = mine.shape[3]
    width = mine.shape[4]
    features = total.shape[1]
    place = (n, last - n)
    onward = (jnp.minimum(n + 1, last), jnp.maximum(n - 1, 0))
    back = (jnp.maximum(n - 1, 0), jnp.minimum(n + 1, last))

    @pl.when(tick == 0)
    def _():
        barrier = pltpu.get_barrier_semaphore()

        @pl.when(n > 0)
        def _():
            pl.semaphore_signal(barrier, inc=1, device_id={"narrow": n - 1})

        @pl.when(n < last)
        def _():
            pl.semaphore_signal(barrier, inc=1, device_id={"narrow": n + 1})

        inner = (n > 0) & (n < last)

        @pl.when(inner)
        def _():
            pl.semaphore_wait(barrier, 2)

        @pl.when(jnp.logical_not(inner))
        def _():
            pl.semaphore_wait(barrier, 1)

    def down_copy(c):
        return pltpu.make_async_copy(
            down_ref.at[pl.ds(pl.multiple_of(c * width, width), width)],
            down_held.at[c],
            down_sem.at[c],
        )

    ahead = tick - LAG * last

    @pl.when((ahead >= 0) & (ahead < chunks))
    def _():
        down_copy(ahead).start()

    @pl.when(tick < chunks)
    def _():
        piece = piece_ref[...]
        gate = jnp.dot(piece, gate_ref[...], preferred_element_type=jnp.float32)
        up = jnp.dot(piece, up_ref[...], preferred_element_type=jnp.float32)
        for way in range(2):
            mine[tick, way, 0] = gate[way * rows : (way + 1) * rows].astype(jnp.bfloat16)
            mine[tick, way, 1] = up[way * rows : (way + 1) * rows].astype(jnp.bfloat16)

    def sum_copy(c, way):
        return pltpu.make_async_remote_copy(
            src_ref=mine.at[c, way],
            dst_ref=arrived.at[c, way],
            send_sem=sum_send.at[c, way],
            recv_sem=sum_recv.at[c, way],
            device_id={"narrow": onward[way]},
        )

    def hid_copy(c, way):
        return pltpu.make_async_remote_copy(
            src_ref=hidden.at[c, way],
            dst_ref=hidden.at[c, way],
            send_sem=hid_send.at[c, way],
            recv_sem=hid_recv.at[c, way],
            device_id={"narrow": back[way]},
        )

    for way in range(2):
        at = place[way]
        c = tick - LAG * at
        active = (c >= 0) & (c < chunks)

        @pl.when(active & (at > 0))
        def _():
            sum_copy(c, way).wait_recv()

        @pl.when(active & (at > 0) & (at < last))
        def _():
            mine[c, way] = (
                mine[c, way].astype(jnp.float32) + arrived[c, way].astype(jnp.float32)
            ).astype(jnp.bfloat16)

        @pl.when(active & (at < last))
        def _():
            sum_copy(c, way).start()

        @pl.when(active & (at == last))
        def _():
            gate = mine[c, way, 0].astype(jnp.float32) + arrived[c, way, 0].astype(jnp.float32)
            up = mine[c, way, 1].astype(jnp.float32) + arrived[c, way, 1].astype(jnp.float32)
            hidden[c, way] = (jax.nn.silu(gate) * up).astype(jnp.bfloat16)
            hid_copy(c, way).start()

        b = tick - LAG * last - LAG * (last - at)
        relayed = (b >= 0) & (b < chunks) & (at < last)

        @pl.when(relayed)
        def _():
            hid_copy(b, way).wait_recv()

        @pl.when(relayed & (at > 0))
        def _():
            hid_copy(b, way).start()

    ready = tick - LAG * 2 * last

    @pl.when((ready >= 0) & (ready < chunks))
    def _():
        down_copy(ready).wait()
        left = hidden[ready].reshape(2 * rows, width)
        tile = 512

        def add(j, carry):
            columns = pl.ds(pl.multiple_of(j * tile, tile), tile)
            term = jnp.dot(left, down_held[ready, :, columns], preferred_element_type=jnp.float32)

            @pl.when(ready == 0)
            def _():
                total[:, columns] = term

            @pl.when(ready > 0)
            def _():
                total[:, columns] += term

            return carry

        lax.fori_loop(0, features // tile, add, 0)

    @pl.when(tick == ticks - 1)
    def _():
        for way in range(2):
            at = place[way]

            def ended(c, carry):
                @pl.when(at < last)
                def _():
                    sum_copy(c, way).wait_send()

                @pl.when(at > 0)
                def _():
                    hid_copy(c, way).wait_send()

                return carry

            lax.fori_loop(0, chunks, ended, 0)
        share = features // wide
        for k in range(wide):
            out_ref[k] = total[:, k * share : (k + 1) * share].astype(jnp.bfloat16)


def scatter_kernel(
    wide, narrow, term_ref, out_ref,
    near, held, far, summed, parts, landed,
    c_send, c_recv, w_send, w_recv, a_send, a_recv,
):
    w = lax.axis_index("wide")
    n = lax.axis_index("narrow")
    me = w * narrow + n
    devices = wide * narrow
    chips = wide // 2
    core = w % 2
    chip = w // 2
    rows = term_ref.shape[1]
    half = rows // 2
    own_rows = rows // devices
    share = term_ref.shape[2]
    orders = bit_orders(chips)
    steps = chips.bit_length() - 1
    barrier = pltpu.get_barrier_semaphore()

    def greet(i, carry):
        peer = (me + i) % devices
        pl.semaphore_signal(
            barrier, inc=1, device_id={"wide": peer // narrow, "narrow": peer % narrow}
        )
        return carry

    lax.fori_loop(1, devices, greet, 0)
    pl.semaphore_wait(barrier, devices - 1)

    def core_copy(k):
        return pltpu.make_async_remote_copy(
            src_ref=term_ref.at[2 * k + 1 - core],
            dst_ref=near.at[k],
            send_sem=c_send.at[k],
            recv_sem=c_recv.at[k],
            device_id={"wide": flip(w, 0)},
        )

    for k in range(chips):
        core_copy(k).start()
    for k in range(chips):
        core_copy(k).wait_recv()
        held[k] = (
            term_ref[2 * k + core].astype(jnp.float32) + near[k].astype(jnp.float32)
        ).astype(jnp.bfloat16)

    def chip_copy(block, part, step, number, to):
        span = pl.ds(part * half, half)
        return pltpu.make_async_remote_copy(
            src_ref=held.at[block, span],
            dst_ref=far.at[step, block, span],
            send_sem=w_send.at[part, number],
            recv_sem=w_recv.at[part, number],
            device_id={"wide": 2 * to + core},
        )

    sends = []
    number = 0
    for step in range(steps):
        for part in range(2):
            order = orders[part]
            to = flip(chip, order[step])
            for k, block in enumerate(flips(to, order[step + 1 :])):
                copy = chip_copy(block, part, step, number + k, to)
                copy.start()
                sends.append(copy)
        for part in range(2):
            order = orders[part]
            to = flip(chip, order[step])
            span = pl.ds(part * half, half)
            for k, block in enumerate(flips(chip, order[step + 1 :])):
                chip_copy(block, part, step, number + k, to).wait_recv()
                value = held[block, span].astype(jnp.float32) + far[step, block, span].astype(
                    jnp.float32
                )
                if step < steps - 1:
                    held[block, span] = value.astype(jnp.bfloat16)
                else:
                    summed[span] = value
        number += 2 ** (steps - 1 - step)

    for i in range(devices):
        parts[i] = summed[i * own_rows : (i + 1) * own_rows].astype(jnp.bfloat16)

    def part_copy(to, source):
        return pltpu.make_async_remote_copy(
            src_ref=parts.at[to],
            dst_ref=landed.at[source],
            send_sem=a_send.at[to],
            recv_sem=a_recv.at[source],
            device_id={"wide": to // narrow, "narrow": to % narrow},
        )

    def send(i, carry):
        part_copy((me + i) % devices, me).start()
        return carry

    lax.fori_loop(1, devices, send, 0)
    landed[me] = parts[me]
    for k in range(chips):
        core_copy(k).wait_send()
    for copy in sends:
        copy.wait_send()

    def finish(i, carry):
        other = (me + i) % devices
        part_copy(other, other).wait_recv()
        part_copy(other, other).wait_send()
        return carry

    lax.fori_loop(1, devices, finish, 0)
    for i in range(wide):
        for j in range(narrow):
            start = (j * wide + i) * share
            out_ref[:, start : start + share] = landed[i * narrow + j]


def per_device(
    wide,
    narrow,
    residual,
    queries,
    keys,
    values,
    cache_lengths,
    track_numbers,
    track_table,
    norm_gain,
    gate_weight,
    up_weight,
    down_weight,
):
    batch_rows, model = residual.shape
    key_heads = keys.shape[1]
    cache_size = keys.shape[2]
    head_size = keys.shape[3]
    grouped = queries.reshape(batch_rows, key_heads, -1, head_size)
    scores = jnp.einsum(
        "bkgd,bkld->bkgl", grouped, keys, preferred_element_type=jnp.float32
    ) / math.sqrt(head_size)
    visible = jnp.arange(cache_size, dtype=jnp.int32)[None, :] < cache_lengths[:, None]
    scores = jnp.where(visible[:, None, None, :], scores, -jnp.inf)
    highest = jnp.max(scores, axis=-1, keepdims=True)
    weights = jnp.exp(scores - highest)
    probs = (weights / jnp.sum(weights, axis=-1, keepdims=True)).astype(jnp.bfloat16)
    context = jnp.einsum(
        "bkgl,bkld->bkgd", probs, values, preferred_element_type=jnp.float32
    ).reshape(batch_rows, -1)
    one_hot = (
        track_numbers[:, None] == jnp.arange(track_table.shape[0], dtype=jnp.int32)[None, :]
    ).astype(jnp.bfloat16)
    stream = (
        residual.astype(jnp.float32)
        + context
        + jnp.dot(one_hot, track_table, preferred_element_type=jnp.float32)
    )
    attended = stream.astype(jnp.bfloat16)
    scale = lax.rsqrt(jnp.mean(stream * stream, axis=-1, keepdims=True) + 1e-05)
    normed = (stream * scale * norm_gain.astype(jnp.float32)).astype(jnp.bfloat16)

    depth = model // narrow
    devices = wide * narrow
    rows = batch_rows * devices
    vmem = pl.BlockSpec(memory_space=pltpu.VMEM)
    dma = pltpu.SemaphoreType.DMA
    bf16 = jnp.bfloat16
    split = normed.reshape(batch_rows, narrow, depth).transpose(1, 0, 2)
    gathered = pl.pallas_call(
        functools.partial(gather_kernel, wide, narrow),
        out_shape=jax.ShapeDtypeStruct((wide, narrow, batch_rows, depth), bf16),
        in_specs=[vmem],
        out_specs=vmem,
        scratch_shapes=[
            pltpu.VMEM((wide, narrow, batch_rows, depth), bf16),
            dma(()),
            dma((narrow,)),
            dma((narrow,)),
            dma((2, wide)),
            dma((2, wide)),
        ],
        compiler_params=pltpu.CompilerParams(
            collective_id=0, has_side_effects=True, vmem_limit_bytes=VMEM_LIMIT
        ),
        name="gather",
    )(split)
    piece = gathered.reshape(rows, depth)

    columns = gate_weight.shape[1]
    width = 256 if columns % 256 == 0 else 128
    chunks = columns // width
    ticks = chunks + LAG * 2 * (narrow - 1)
    share = depth // wide
    term = pl.pallas_call(
        functools.partial(ffn_kernel, wide, narrow, chunks, ticks),
        grid=(ticks,),
        out_shape=jax.ShapeDtypeStruct((wide, rows, share), bf16),
        in_specs=[
            pl.BlockSpec((rows, depth), lambda i: (0, 0)),
            pl.BlockSpec((depth, width), lambda i: (0, jnp.minimum(i, chunks - 1))),
            pl.BlockSpec((depth, width), lambda i: (0, jnp.minimum(i, chunks - 1))),
            pl.BlockSpec(memory_space=pl.ANY),
        ],
        out_specs=pl.BlockSpec((wide, rows, share), lambda i: (0, 0, 0)),
        scratch_shapes=[
            pltpu.VMEM((chunks, 2, 2, rows // 2, width), bf16),
            pltpu.VMEM((chunks, 2, 2, rows // 2, width), bf16),
            pltpu.VMEM((chunks, 2, rows // 2, width), bf16),
            pltpu.VMEM((rows, depth), jnp.float32),
            pltpu.VMEM((chunks, width, depth), bf16),
            dma((chunks, 2)),
            dma((chunks, 2)),
            dma((chunks, 2)),
            dma((chunks, 2)),
            dma((chunks,)),
        ],
        compiler_params=pltpu.CompilerParams(
            collective_id=1, has_side_effects=True, vmem_limit_bytes=VMEM_LIMIT
        ),
        name="ffn",
    )(piece, gate_weight, up_weight, down_weight)

    chips = wide // 2
    steps = chips.bit_length() - 1
    ffn_out = pl.pallas_call(
        functools.partial(scatter_kernel, wide, narrow),
        out_shape=jax.ShapeDtypeStruct((batch_rows, model), bf16),
        in_specs=[vmem],
        out_specs=vmem,
        scratch_shapes=[
            pltpu.VMEM((chips, rows, share), bf16),
            pltpu.VMEM((chips, rows, share), bf16),
            pltpu.VMEM((steps, chips, rows, share), bf16),
            pltpu.VMEM((rows, share), jnp.float32),
            pltpu.VMEM((devices, batch_rows, share), bf16),
            pltpu.VMEM((devices, batch_rows, share), bf16),
            dma((chips,)),
            dma((chips,)),
            dma((2, chips)),
            dma((2, chips)),
            dma((devices,)),
            dma((devices,)),
        ],
        compiler_params=pltpu.CompilerParams(
            collective_id=2, has_side_effects=True, vmem_limit_bytes=VMEM_LIMIT
        ),
        name="scatter",
    )(term)
    return (attended, ffn_out)


def solution(mesh):
    in_specs = (
        P(("wide", "narrow"), None),
        P(("wide", "narrow"), None),
        P(("wide", "narrow"), None, None, None),
        P(("wide", "narrow"), None, None, None),
        P(("wide", "narrow")),
        P(("wide", "narrow")),
        P(),
        P(),
        P("narrow", "wide"),
        P("narrow", "wide"),
        P("wide", "narrow"),
    )
    out_specs = (P(("wide", "narrow"), None), P(("wide", "narrow"), None))
    return jax.shard_map(
        functools.partial(per_device, mesh.shape["wide"], mesh.shape["narrow"]),
        mesh=mesh,
        in_specs=in_specs,
        out_specs=out_specs,
        check_vma=False,
    )
```

```python
import functools
import math

import jax
import jax.numpy as jnp
from jax import lax
from jax.experimental import pallas as pl
from jax.experimental.pallas import tpu as pltpu
from jax.sharding import PartitionSpec as P

LAG = 2
BACK = 1
VMEM_LIMIT = 66_000_000


def flip(index, bit):
    step = 2**bit
    return index + step * (1 - 2 * ((index // step) % 2))


def flips(index, bits):
    found = [index]
    for bit in bits:
        found = found + [flip(one, bit) for one in found]
    return found


def bit_orders(chips):
    count = chips.bit_length() - 1
    bits = list(range(count))
    half = count // 2
    return (bits, bits[half:] + bits[:half])


def meet(peers):
    barrier = pltpu.get_barrier_semaphore()
    for peer in peers:
        pl.semaphore_signal(barrier, inc=1, device_id=peer)
    pl.semaphore_wait(barrier, len(peers))


def gather_kernel(wide, narrow, mine_ref, out_ref, held, own_sem, z_send, z_recv, w_send, w_recv):
    w = lax.axis_index("wide")
    n = lax.axis_index("narrow")
    chips = wide // 2
    orders = bit_orders(chips)
    half = narrow // 2
    steps = wide.bit_length() - 1
    meet(
        [{"narrow": (n + i) % narrow} for i in range(1, narrow)]
        + [{"wide": flip(w, bit)} for bit in range(steps)]
    )

    own = pltpu.make_async_copy(mine_ref.at[n], held.at[w, n], own_sem)
    own.start()
    sends = []
    for i in range(1, narrow):
        to = (n + i) % narrow
        copy = pltpu.make_async_remote_copy(
            src_ref=mine_ref.at[to],
            dst_ref=held.at[w, n],
            send_sem=z_send.at[i],
            recv_sem=z_recv.at[n],
            device_id={"narrow": to},
        )
        copy.start()
        sends.append(copy)
    own.wait()
    for i in range(1, narrow):
        source = (n + i) % narrow
        pltpu.make_async_remote_copy(
            src_ref=mine_ref.at[source],
            dst_ref=held.at[w, source],
            send_sem=z_send.at[i],
            recv_sem=z_recv.at[source],
            device_id={"narrow": source},
        ).wait_recv()

    def block_copy(block, part, number, to):
        return pltpu.make_async_remote_copy(
            src_ref=held.at[block, pl.ds(part * half, half)],
            dst_ref=held.at[block, pl.ds(part * half, half)],
            send_sem=w_send.at[part, number],
            recv_sem=w_recv.at[part, block],
            device_id={"wide": to},
        )

    walks = [[bit + 1 for bit in order] + [0] for order in orders]
    number = 0
    for step in range(steps):
        for part in range(2):
            walk = walks[part]
            to = flip(w, walk[step])
            for k, block in enumerate(flips(w, walk[:step])):
                copy = block_copy(block, part, number + k, to)
                copy.start()
                sends.append(copy)
        for part in range(2):
            walk = walks[part]
            to = flip(w, walk[step])
            for k, block in enumerate(flips(to, walk[:step])):
                block_copy(block, part, number + k, to).wait_recv()
        number += 2**step
    for copy in sends:
        copy.wait_send()
    out_ref[...] = held[...]


def ffn_kernel(
    wide, narrow, chunks, ticks,
    piece_ref, gate_ref, up_ref, down_ref, keep_ref, give_ref,
    mine, sent, arrived, hidden, total, down_held,
    sum_send, sum_recv, hid_send, hid_recv, down_sem,
):
    tick = pl.program_id(0)
    n = lax.axis_index("narrow")
    last = narrow - 1
    rows = mine.shape[3]
    width = mine.shape[4]
    slots = mine.shape[0]
    place = (n, last - n)
    onward = (jnp.minimum(n + 1, last), jnp.maximum(n - 1, 0))
    back = (jnp.maximum(n - 1, 0), jnp.minimum(n + 1, last))

    @pl.when(tick == 0)
    def _():
        barrier = pltpu.get_barrier_semaphore()

        @pl.when(n > 0)
        def _():
            pl.semaphore_signal(barrier, inc=1, device_id={"narrow": n - 1})

        @pl.when(n < last)
        def _():
            pl.semaphore_signal(barrier, inc=1, device_id={"narrow": n + 1})

        inner = (n > 0) & (n < last)

        @pl.when(inner)
        def _():
            pl.semaphore_wait(barrier, 2)

        @pl.when(jnp.logical_not(inner))
        def _():
            pl.semaphore_wait(barrier, 1)

    def down_copy(c):
        return pltpu.make_async_copy(
            down_ref.at[pl.ds(pl.multiple_of(c * width, width), width)],
            down_held.at[c],
            down_sem.at[c],
        )

    ahead = tick - LAG * last

    @pl.when((ahead >= 0) & (ahead < chunks))
    def _():
        down_copy(ahead).start()

    @pl.when(tick < chunks)
    def _():
        piece = piece_ref[...]
        gate = jnp.dot(piece, gate_ref[...], preferred_element_type=jnp.float32)
        up = jnp.dot(piece, up_ref[...], preferred_element_type=jnp.float32)
        for way in range(2):
            mine[tick % slots, way, 0] = gate[way * rows : (way + 1) * rows]
            mine[tick % slots, way, 1] = up[way * rows : (way + 1) * rows]

    def sum_copy(c, way):
        return pltpu.make_async_remote_copy(
            src_ref=sent.at[c, way],
            dst_ref=arrived.at[c, way],
            send_sem=sum_send.at[c, way],
            recv_sem=sum_recv.at[c, way],
            device_id={"narrow": onward[way]},
        )

    def hid_copy(c, way):
        return pltpu.make_async_remote_copy(
            src_ref=hidden.at[c, way],
            dst_ref=hidden.at[c, way],
            send_sem=hid_send.at[c, way],
            recv_sem=hid_recv.at[c, way],
            device_id={"narrow": back[way]},
        )

    for way in range(2):
        at = place[way]
        c = tick - LAG * at
        active = (c >= 0) & (c < chunks)

        @pl.when(active & (at > 0))
        def _():
            sum_copy(c, way).wait_recv()

        slot = (c + slots) % slots

        @pl.when(active & (at == 0))
        def _():
            sent[c, way] = mine[slot, way].astype(jnp.bfloat16)

        @pl.when(active & (at > 0) & (at < last))
        def _():
            sent[c, way] = (mine[slot, way] + arrived[c, way].astype(jnp.float32)).astype(
                jnp.bfloat16
            )

        @pl.when(active & (at < last))
        def _():
            sum_copy(c, way).start()

        @pl.when(active & (at == last))
        def _():
            gate = mine[slot, way, 0] + arrived[c, way, 0].astype(jnp.float32)
            up = mine[slot, way, 1] + arrived[c, way, 1].astype(jnp.float32)
            hidden[c, way] = (jax.nn.silu(gate) * up).astype(jnp.bfloat16)
            hid_copy(c, way).start()

        b = tick - LAG * last - BACK * (last - at)
        relayed = (b >= 0) & (b < chunks) & (at < last)

        @pl.when(relayed)
        def _():
            hid_copy(b, way).wait_recv()

        @pl.when(relayed & (at > 0))
        def _():
            hid_copy(b, way).start()

    ready = tick - (LAG + BACK) * last

    @pl.when((ready >= 0) & (ready < chunks))
    def _():
        down_copy(ready).wait()
        left = hidden[ready].reshape(2 * rows, width)
        share = total.shape[2]

        def add(j, carry):
            columns = pl.ds(pl.multiple_of(j * share, share), share)
            term = jnp.dot(left, down_held[ready, :, columns], preferred_element_type=jnp.float32)

            @pl.when(ready == 0)
            def _():
                total[j] = term

            @pl.when(ready > 0)
            def _():
                total[j] += term

            return carry

        lax.fori_loop(0, wide, add, 0)

    @pl.when(tick == ticks - 1)
    def _():
        for way in range(2):
            at = place[way]

            def ended(c, carry):
                @pl.when(at < last)
                def _():
                    sum_copy(c, way).wait_send()

                @pl.when(at > 0)
                def _():
                    hid_copy(c, way).wait_send()

                return carry

            lax.fori_loop(0, chunks, ended, 0)
        core = lax.axis_index("wide") % 2
        for k in range(wide // 2):
            keep_ref[k] = total[2 * k + core]
            give_ref[k] = total[2 * k + 1 - core].astype(jnp.bfloat16)


def scatter_kernel(
    wide, narrow, keep_ref, give_ref, out_ref,
    near, held, wire, far, summed, parts, landed,
    c_send, c_recv, w_send, w_recv, a_send, a_recv,
):
    w = lax.axis_index("wide")
    n = lax.axis_index("narrow")
    me = w * narrow + n
    devices = wide * narrow
    chips = wide // 2
    core = w % 2
    chip = w // 2
    rows = keep_ref.shape[1]
    half = rows // 2
    own_rows = rows // devices
    share = keep_ref.shape[2]
    orders = bit_orders(chips)
    steps = chips.bit_length() - 1
    barrier = pltpu.get_barrier_semaphore()

    def greet(i, carry):
        peer = (me + i) % devices
        pl.semaphore_signal(
            barrier, inc=1, device_id={"wide": peer // narrow, "narrow": peer % narrow}
        )
        return carry

    lax.fori_loop(1, devices, greet, 0)
    pl.semaphore_wait(barrier, devices - 1)

    def core_copy(k):
        return pltpu.make_async_remote_copy(
            src_ref=give_ref.at[k],
            dst_ref=near.at[k],
            send_sem=c_send.at[k],
            recv_sem=c_recv.at[k],
            device_id={"wide": flip(w, 0)},
        )

    for k in range(chips):
        core_copy(k).start()
    for k in range(chips):
        core_copy(k).wait_recv()
        held[k] = keep_ref[k] + near[k].astype(jnp.float32)

    def chip_copy(block, part, step, number, to):
        span = pl.ds(part * half, half)
        return pltpu.make_async_remote_copy(
            src_ref=wire.at[block, span],
            dst_ref=far.at[step, block, span],
            send_sem=w_send.at[part, number],
            recv_sem=w_recv.at[part, number],
            device_id={"wide": 2 * to + core},
        )

    sends = []
    number = 0
    for step in range(steps):
        for part in range(2):
            order = orders[part]
            to = flip(chip, order[step])
            for k, block in enumerate(flips(to, order[step + 1 :])):
                span = pl.ds(part * half, half)
                wire[block, span] = held[block, span].astype(jnp.bfloat16)
                copy = chip_copy(block, part, step, number + k, to)
                copy.start()
                sends.append(copy)
        for part in range(2):
            order = orders[part]
            to = flip(chip, order[step])
            span = pl.ds(part * half, half)
            for k, block in enumerate(flips(chip, order[step + 1 :])):
                chip_copy(block, part, step, number + k, to).wait_recv()
                value = held[block, span] + far[step, block, span].astype(
                    jnp.float32
                )
                if step < steps - 1:
                    held[block, span] = value
                else:
                    summed[span] = value
        number += 2 ** (steps - 1 - step)

    for i in range(devices):
        parts[i] = summed[i * own_rows : (i + 1) * own_rows].astype(jnp.bfloat16)

    def part_copy(to, source):
        return pltpu.make_async_remote_copy(
            src_ref=parts.at[to],
            dst_ref=landed.at[source],
            send_sem=a_send.at[to],
            recv_sem=a_recv.at[source],
            device_id={"wide": to // narrow, "narrow": to % narrow},
        )

    def send(i, carry):
        part_copy((me + i) % devices, me).start()
        return carry

    lax.fori_loop(1, devices, send, 0)
    landed[me] = parts[me]
    for k in range(chips):
        core_copy(k).wait_send()
    for copy in sends:
        copy.wait_send()

    def finish(i, carry):
        other = (me + i) % devices
        part_copy(other, other).wait_recv()
        part_copy(other, other).wait_send()
        return carry

    lax.fori_loop(1, devices, finish, 0)
    for i in range(wide):
        for j in range(narrow):
            start = (j * wide + i) * share
            out_ref[:, start : start + share] = landed[i * narrow + j]


def per_device(
    wide,
    narrow,
    residual,
    queries,
    keys,
    values,
    cache_lengths,
    track_numbers,
    track_table,
    norm_gain,
    gate_weight,
    up_weight,
    down_weight,
):
    batch_rows, model = residual.shape
    key_heads = keys.shape[1]
    cache_size = keys.shape[2]
    head_size = keys.shape[3]
    grouped = queries.reshape(batch_rows, key_heads, -1, head_size)
    scores = jnp.einsum(
        "bkgd,bkld->bkgl", grouped, keys, preferred_element_type=jnp.float32
    ) / math.sqrt(head_size)
    visible = jnp.arange(cache_size, dtype=jnp.int32)[None, :] < cache_lengths[:, None]
    scores = jnp.where(visible[:, None, None, :], scores, -jnp.inf)
    highest = jnp.max(scores, axis=-1, keepdims=True)
    weights = jnp.exp(scores - highest)
    probs = (weights / jnp.sum(weights, axis=-1, keepdims=True)).astype(jnp.bfloat16)
    context = jnp.einsum(
        "bkgl,bkld->bkgd", probs, values, preferred_element_type=jnp.float32
    ).reshape(batch_rows, -1)
    one_hot = (
        track_numbers[:, None] == jnp.arange(track_table.shape[0], dtype=jnp.int32)[None, :]
    ).astype(jnp.bfloat16)
    stream = (
        residual.astype(jnp.float32)
        + context
        + jnp.dot(one_hot, track_table, preferred_element_type=jnp.float32)
    )
    attended = stream.astype(jnp.bfloat16)
    scale = lax.rsqrt(jnp.mean(stream * stream, axis=-1, keepdims=True) + 1e-05)
    normed = (stream * scale * norm_gain.astype(jnp.float32)).astype(jnp.bfloat16)

    depth = model // narrow
    devices = wide * narrow
    rows = batch_rows * devices
    vmem = pl.BlockSpec(memory_space=pltpu.VMEM)
    dma = pltpu.SemaphoreType.DMA
    bf16 = jnp.bfloat16
    lines = batch_rows * depth // 128
    split = (
        normed.reshape(batch_rows, narrow, depth // 128, 128)
        .transpose(1, 0, 2, 3)
        .reshape(narrow, lines, 128)
    )
    gathered = pl.pallas_call(
        functools.partial(gather_kernel, wide, narrow),
        out_shape=jax.ShapeDtypeStruct((wide, narrow, lines, 128), bf16),
        in_specs=[vmem],
        out_specs=vmem,
        scratch_shapes=[
            pltpu.VMEM((wide, narrow, lines, 128), bf16),
            dma(()),
            dma((narrow,)),
            dma((narrow,)),
            dma((2, wide)),
            dma((2, wide)),
        ],
        compiler_params=pltpu.CompilerParams(
            collective_id=0, has_side_effects=True, vmem_limit_bytes=VMEM_LIMIT
        ),
        name="gather",
    )(split)
    piece = gathered.reshape(rows, depth)

    columns = gate_weight.shape[1]
    width = 256 if columns % 256 == 0 else 128
    chunks = columns // width
    slots = LAG * (narrow - 1) + 1
    ticks = chunks + (LAG + BACK) * (narrow - 1)
    chips = wide // 2
    share = depth // wide
    keep, give = pl.pallas_call(
        functools.partial(ffn_kernel, wide, narrow, chunks, ticks),
        grid=(ticks,),
        out_shape=(
            jax.ShapeDtypeStruct((chips, rows, share), jnp.float32),
            jax.ShapeDtypeStruct((chips, rows, share), bf16),
        ),
        in_specs=[
            pl.BlockSpec((rows, depth), lambda i: (0, 0), pipeline_mode=pl.Buffered(1)),
            pl.BlockSpec((depth, width), lambda i: (0, jnp.minimum(i, chunks - 1))),
            pl.BlockSpec((depth, width), lambda i: (0, jnp.minimum(i, chunks - 1))),
            pl.BlockSpec(memory_space=pl.ANY),
        ],
        out_specs=(pl.BlockSpec((chips, rows, share), lambda i: (0, 0, 0)),) * 2,
        scratch_shapes=[
            pltpu.VMEM((slots, 2, 2, rows // 2, width), jnp.float32),
            pltpu.VMEM((chunks, 2, 2, rows // 2, width), bf16),
            pltpu.VMEM((chunks, 2, 2, rows // 2, width), bf16),
            pltpu.VMEM((chunks, 2, rows // 2, width), bf16),
            pltpu.VMEM((wide, rows, share), jnp.float32),
            pltpu.VMEM((chunks, width, depth), bf16),
            dma((chunks, 2)),
            dma((chunks, 2)),
            dma((chunks, 2)),
            dma((chunks, 2)),
            dma((chunks,)),
        ],
        compiler_params=pltpu.CompilerParams(
            collective_id=1, has_side_effects=True, vmem_limit_bytes=VMEM_LIMIT
        ),
        name="ffn",
    )(piece, gate_weight, up_weight, down_weight)

    steps = chips.bit_length() - 1
    ffn_out = pl.pallas_call(
        functools.partial(scatter_kernel, wide, narrow),
        out_shape=jax.ShapeDtypeStruct((batch_rows, model), bf16),
        in_specs=[vmem, vmem],
        out_specs=vmem,
        scratch_shapes=[
            pltpu.VMEM((chips, rows, share), bf16),
            pltpu.VMEM((chips, rows, share), jnp.float32),
            pltpu.VMEM((chips, rows, share), bf16),
            pltpu.VMEM((steps, chips, rows, share), bf16),
            pltpu.VMEM((rows, share), jnp.float32),
            pltpu.VMEM((devices, batch_rows, share), bf16),
            pltpu.VMEM((devices, batch_rows, share), bf16),
            dma((chips,)),
            dma((chips,)),
            dma((2, chips)),
            dma((2, chips)),
            dma((devices,)),
            dma((devices,)),
        ],
        compiler_params=pltpu.CompilerParams(
            collective_id=2, has_side_effects=True, vmem_limit_bytes=VMEM_LIMIT
        ),
        name="scatter",
    )(keep, give)
    return (attended, ffn_out)


def solution(mesh):
    in_specs = (
        P(("wide", "narrow"), None),
        P(("wide", "narrow"), None),
        P(("wide", "narrow"), None, None, None),
        P(("wide", "narrow"), None, None, None),
        P(("wide", "narrow")),
        P(("wide", "narrow")),
        P(),
        P(),
        P("narrow", "wide"),
        P("narrow", "wide"),
        P("wide", "narrow"),
    )
    out_specs = (P(("wide", "narrow"), None), P(("wide", "narrow"), None))
    return jax.shard_map(
        functools.partial(per_device, mesh.shape["wide"], mesh.shape["narrow"]),
        mesh=mesh,
        in_specs=in_specs,
        out_specs=out_specs,
        check_vma=False,
    )
```

```python
import functools
import math

import jax
import jax.numpy as jnp
from jax import lax
from jax.experimental import pallas as pl
from jax.experimental.pallas import tpu as pltpu
from jax.sharding import PartitionSpec as P

LAG = 2
BACK = 2
VMEM_LIMIT = 66_000_000


def flip(index, bit):
    step = 2**bit
    return index + step * (1 - 2 * ((index // step) % 2))


def flips(index, bits):
    found = [index]
    for bit in bits:
        found = found + [flip(one, bit) for one in found]
    return found


def bit_orders(chips):
    count = chips.bit_length() - 1
    bits = list(range(count))
    half = count // 2
    return (bits, bits[half:] + bits[:half])


def meet(peers):
    barrier = pltpu.get_barrier_semaphore()
    for peer in peers:
        pl.semaphore_signal(barrier, inc=1, device_id=peer)
    pl.semaphore_wait(barrier, len(peers))


def gather_kernel(wide, narrow, mine_ref, out_ref, held, own_sem, z_send, z_recv, w_send, w_recv):
    w = lax.axis_index("wide")
    n = lax.axis_index("narrow")
    chips = wide // 2
    orders = bit_orders(chips)
    half = narrow // 2
    steps = wide.bit_length() - 1
    meet(
        [{"narrow": (n + i) % narrow} for i in range(1, narrow)]
        + [{"wide": flip(w, bit)} for bit in range(steps)]
    )

    own = pltpu.make_async_copy(mine_ref.at[n], held.at[w, n], own_sem)
    own.start()
    sends = []
    for i in range(1, narrow):
        to = (n + i) % narrow
        copy = pltpu.make_async_remote_copy(
            src_ref=mine_ref.at[to],
            dst_ref=held.at[w, n],
            send_sem=z_send.at[i],
            recv_sem=z_recv.at[n],
            device_id={"narrow": to},
        )
        copy.start()
        sends.append(copy)
    own.wait()
    for i in range(1, narrow):
        source = (n + i) % narrow
        pltpu.make_async_remote_copy(
            src_ref=mine_ref.at[source],
            dst_ref=held.at[w, source],
            send_sem=z_send.at[i],
            recv_sem=z_recv.at[source],
            device_id={"narrow": source},
        ).wait_recv()

    def block_copy(block, part, number, to):
        return pltpu.make_async_remote_copy(
            src_ref=held.at[block, pl.ds(part * half, half)],
            dst_ref=held.at[block, pl.ds(part * half, half)],
            send_sem=w_send.at[part, number],
            recv_sem=w_recv.at[part, block],
            device_id={"wide": to},
        )

    walks = [[bit + 1 for bit in order] + [0] for order in orders]
    number = 0
    for step in range(steps):
        for part in range(2):
            walk = walks[part]
            to = flip(w, walk[step])
            for k, block in enumerate(flips(w, walk[:step])):
                copy = block_copy(block, part, number + k, to)
                copy.start()
                sends.append(copy)
        for part in range(2):
            walk = walks[part]
            to = flip(w, walk[step])
            for k, block in enumerate(flips(to, walk[:step])):
                block_copy(block, part, number + k, to).wait_recv()
        number += 2**step
    for copy in sends:
        copy.wait_send()
    out_ref[...] = held[...]


def ffn_kernel(
    wide, narrow, chunks, ticks,
    piece_ref, gate_ref, up_ref, down_ref, keep_ref, give_ref,
    mine, sent, arrived, hidden, total, down_held,
    sum_send, sum_recv, hid_send, hid_recv, down_sem,
):
    tick = pl.program_id(0)
    n = lax.axis_index("narrow")
    last = narrow - 1
    rows = mine.shape[3]
    width = mine.shape[4]
    slots = mine.shape[0]
    place = (n, last - n)
    onward = (jnp.minimum(n + 1, last), jnp.maximum(n - 1, 0))
    back = (jnp.maximum(n - 1, 0), jnp.minimum(n + 1, last))

    @pl.when(tick == 0)
    def _():
        barrier = pltpu.get_barrier_semaphore()

        @pl.when(n > 0)
        def _():
            pl.semaphore_signal(barrier, inc=1, device_id={"narrow": n - 1})

        @pl.when(n < last)
        def _():
            pl.semaphore_signal(barrier, inc=1, device_id={"narrow": n + 1})

        inner = (n > 0) & (n < last)

        @pl.when(inner)
        def _():
            pl.semaphore_wait(barrier, 2)

        @pl.when(jnp.logical_not(inner))
        def _():
            pl.semaphore_wait(barrier, 1)

    def down_copy(c):
        return pltpu.make_async_copy(
            down_ref.at[pl.ds(pl.multiple_of(c * width, width), width)],
            down_held.at[c],
            down_sem.at[c],
        )

    ahead = tick - LAG * last

    @pl.when((ahead >= 0) & (ahead < chunks))
    def _():
        down_copy(ahead).start()

    @pl.when(tick < chunks)
    def _():
        piece = piece_ref[...]
        gate = jnp.dot(piece, gate_ref[...], preferred_element_type=jnp.float32)
        up = jnp.dot(piece, up_ref[...], preferred_element_type=jnp.float32)
        for way in range(2):
            mine[tick % slots, way, 0] = gate[way * rows : (way + 1) * rows]
            mine[tick % slots, way, 1] = up[way * rows : (way + 1) * rows]

    def sum_copy(c, way):
        return pltpu.make_async_remote_copy(
            src_ref=sent.at[c, way],
            dst_ref=arrived.at[c, way],
            send_sem=sum_send.at[c, way],
            recv_sem=sum_recv.at[c, way],
            device_id={"narrow": onward[way]},
        )

    def hid_copy(c, way):
        return pltpu.make_async_remote_copy(
            src_ref=hidden.at[c, way],
            dst_ref=hidden.at[c, way],
            send_sem=hid_send.at[c, way],
            recv_sem=hid_recv.at[c, way],
            device_id={"narrow": back[way]},
        )

    for way in range(2):
        at = place[way]
        c = tick - LAG * at
        active = (c >= 0) & (c < chunks)

        @pl.when(active & (at > 0))
        def _():
            sum_copy(c, way).wait_recv()

        slot = (c + slots) % slots

        @pl.when(active & (at == 0))
        def _():
            sent[c, way] = mine[slot, way].astype(jnp.bfloat16)

        @pl.when(active & (at > 0) & (at < last))
        def _():
            sent[c, way] = (mine[slot, way] + arrived[c, way].astype(jnp.float32)).astype(
                jnp.bfloat16
            )

        @pl.when(active & (at < last))
        def _():
            sum_copy(c, way).start()

        @pl.when(active & (at == last))
        def _():
            gate = mine[slot, way, 0] + arrived[c, way, 0].astype(jnp.float32)
            up = mine[slot, way, 1] + arrived[c, way, 1].astype(jnp.float32)
            hidden[c, way] = (jax.nn.silu(gate) * up).astype(jnp.bfloat16)
            hid_copy(c, way).start()

        b = tick - LAG * last - BACK * (last - at)
        relayed = (b >= 0) & (b < chunks) & (at < last)

        @pl.when(relayed)
        def _():
            hid_copy(b, way).wait_recv()

        @pl.when(relayed & (at > 0))
        def _():
            hid_copy(b, way).start()

    ready = tick - (LAG + BACK) * last

    @pl.when((ready >= 0) & (ready < chunks))
    def _():
        down_copy(ready).wait()
        left = hidden[ready].reshape(2 * rows, width)
        share = total.shape[2]

        def add(j, carry):
            columns = pl.ds(pl.multiple_of(j * share, share), share)
            term = jnp.dot(left, down_held[ready, :, columns], preferred_element_type=jnp.float32)

            @pl.when(ready == 0)
            def _():
                total[j] = term

            @pl.when(ready > 0)
            def _():
                total[j] += term

            return carry

        lax.fori_loop(0, wide, add, 0)

    @pl.when(tick == ticks - 1)
    def _():
        for way in range(2):
            at = place[way]

            def ended(c, carry):
                @pl.when(at < last)
                def _():
                    sum_copy(c, way).wait_send()

                @pl.when(at > 0)
                def _():
                    hid_copy(c, way).wait_send()

                return carry

            lax.fori_loop(0, chunks, ended, 0)
        core = lax.axis_index("wide") % 2
        for k in range(wide // 2):
            keep_ref[k] = total[2 * k + core]
            give_ref[k] = total[2 * k + 1 - core].astype(jnp.bfloat16)


def scatter_kernel(
    wide, narrow, keep_ref, give_ref, out_ref,
    near, held, wire, far, summed, parts, landed,
    c_send, c_recv, w_send, w_recv, a_send, a_recv,
):
    w = lax.axis_index("wide")
    n = lax.axis_index("narrow")
    me = w * narrow + n
    devices = wide * narrow
    chips = wide // 2
    core = w % 2
    chip = w // 2
    rows = keep_ref.shape[1]
    half = rows // 2
    own_rows = rows // devices
    share = keep_ref.shape[2]
    orders = bit_orders(chips)
    steps = chips.bit_length() - 1
    barrier = pltpu.get_barrier_semaphore()

    def greet(i, carry):
        peer = (me + i) % devices
        pl.semaphore_signal(
            barrier, inc=1, device_id={"wide": peer // narrow, "narrow": peer % narrow}
        )
        return carry

    lax.fori_loop(1, devices, greet, 0)
    pl.semaphore_wait(barrier, devices - 1)

    def core_copy(k):
        return pltpu.make_async_remote_copy(
            src_ref=give_ref.at[k],
            dst_ref=near.at[k],
            send_sem=c_send.at[k],
            recv_sem=c_recv.at[k],
            device_id={"wide": flip(w, 0)},
        )

    for k in range(chips):
        core_copy(k).start()
    for k in range(chips):
        core_copy(k).wait_recv()
        held[k] = keep_ref[k] + near[k].astype(jnp.float32)

    def chip_copy(block, part, step, number, to):
        span = pl.ds(part * half, half)
        return pltpu.make_async_remote_copy(
            src_ref=wire.at[block, span],
            dst_ref=far.at[step, block, span],
            send_sem=w_send.at[part, number],
            recv_sem=w_recv.at[part, number],
            device_id={"wide": 2 * to + core},
        )

    sends = []
    number = 0
    for step in range(steps):
        for part in range(2):
            order = orders[part]
            to = flip(chip, order[step])
            for k, block in enumerate(flips(to, order[step + 1 :])):
                span = pl.ds(part * half, half)
                wire[block, span] = held[block, span].astype(jnp.bfloat16)
                copy = chip_copy(block, part, step, number + k, to)
                copy.start()
                sends.append(copy)
        for part in range(2):
            order = orders[part]
            to = flip(chip, order[step])
            span = pl.ds(part * half, half)
            for k, block in enumerate(flips(chip, order[step + 1 :])):
                chip_copy(block, part, step, number + k, to).wait_recv()
                value = held[block, span] + far[step, block, span].astype(
                    jnp.float32
                )
                if step < steps - 1:
                    held[block, span] = value
                else:
                    summed[span] = value
        number += 2 ** (steps - 1 - step)

    for i in range(devices):
        parts[i] = summed[i * own_rows : (i + 1) * own_rows].astype(jnp.bfloat16)

    def part_copy(to, source):
        return pltpu.make_async_remote_copy(
            src_ref=parts.at[to],
            dst_ref=landed.at[source],
            send_sem=a_send.at[to],
            recv_sem=a_recv.at[source],
            device_id={"wide": to // narrow, "narrow": to % narrow},
        )

    def send(i, carry):
        part_copy((me + i) % devices, me).start()
        return carry

    lax.fori_loop(1, devices, send, 0)
    landed[me] = parts[me]
    for k in range(chips):
        core_copy(k).wait_send()
    for copy in sends:
        copy.wait_send()

    def finish(i, carry):
        other = (me + i) % devices
        part_copy(other, other).wait_recv()
        part_copy(other, other).wait_send()
        return carry

    lax.fori_loop(1, devices, finish, 0)
    for i in range(wide):
        for j in range(narrow):
            start = (j * wide + i) * share
            out_ref[:, start : start + share] = landed[i * narrow + j]


def per_device(
    wide,
    narrow,
    residual,
    queries,
    keys,
    values,
    cache_lengths,
    track_numbers,
    track_table,
    norm_gain,
    gate_weight,
    up_weight,
    down_weight,
):
    batch_rows, model = residual.shape
    key_heads = keys.shape[1]
    cache_size = keys.shape[2]
    head_size = keys.shape[3]
    grouped = queries.reshape(batch_rows, key_heads, -1, head_size)
    scores = jnp.einsum(
        "bkgd,bkld->bkgl", grouped, keys, preferred_element_type=jnp.float32
    ) / math.sqrt(head_size)
    visible = jnp.arange(cache_size, dtype=jnp.int32)[None, :] < cache_lengths[:, None]
    scores = jnp.where(visible[:, None, None, :], scores, -jnp.inf)
    highest = jnp.max(scores, axis=-1, keepdims=True)
    weights = jnp.exp(scores - highest)
    probs = (weights / jnp.sum(weights, axis=-1, keepdims=True)).astype(jnp.bfloat16)
    context = jnp.einsum(
        "bkgl,bkld->bkgd", probs, values, preferred_element_type=jnp.float32
    ).reshape(batch_rows, -1)
    one_hot = (
        track_numbers[:, None] == jnp.arange(track_table.shape[0], dtype=jnp.int32)[None, :]
    ).astype(jnp.bfloat16)
    stream = (
        residual.astype(jnp.float32)
        + context
        + jnp.dot(one_hot, track_table, preferred_element_type=jnp.float32)
    )
    attended = stream.astype(jnp.bfloat16)
    scale = lax.rsqrt(jnp.mean(stream * stream, axis=-1, keepdims=True) + 1e-05)
    normed = (stream * scale * norm_gain.astype(jnp.float32)).astype(jnp.bfloat16)

    depth = model // narrow
    devices = wide * narrow
    rows = batch_rows * devices
    vmem = pl.BlockSpec(memory_space=pltpu.VMEM)
    dma = pltpu.SemaphoreType.DMA
    bf16 = jnp.bfloat16
    lines = batch_rows * depth // 128
    split = (
        normed.reshape(batch_rows, narrow, depth // 128, 128)
        .transpose(1, 0, 2, 3)
        .reshape(narrow, lines, 128)
    )
    gathered = pl.pallas_call(
        functools.partial(gather_kernel, wide, narrow),
        out_shape=jax.ShapeDtypeStruct((wide, narrow, lines, 128), bf16),
        in_specs=[vmem],
        out_specs=vmem,
        scratch_shapes=[
            pltpu.VMEM((wide, narrow, lines, 128), bf16),
            dma(()),
            dma((narrow,)),
            dma((narrow,)),
            dma((2, wide)),
            dma((2, wide)),
        ],
        compiler_params=pltpu.CompilerParams(
            collective_id=0, has_side_effects=True, vmem_limit_bytes=VMEM_LIMIT
        ),
        name="gather",
    )(split)
    piece = gathered.reshape(rows, depth)

    columns = gate_weight.shape[1]
    width = 256 if columns % 256 == 0 else 128
    chunks = columns // width
    slots = LAG * (narrow - 1) + 1
    ticks = chunks + (LAG + BACK) * (narrow - 1)
    chips = wide // 2
    share = depth // wide
    keep, give = pl.pallas_call(
        functools.partial(ffn_kernel, wide, narrow, chunks, ticks),
        grid=(ticks,),
        out_shape=(
            jax.ShapeDtypeStruct((chips, rows, share), jnp.float32),
            jax.ShapeDtypeStruct((chips, rows, share), bf16),
        ),
        in_specs=[
            pl.BlockSpec((rows, depth), lambda i: (0, 0), pipeline_mode=pl.Buffered(1)),
            pl.BlockSpec((depth, width), lambda i: (0, jnp.minimum(i, chunks - 1))),
            pl.BlockSpec((depth, width), lambda i: (0, jnp.minimum(i, chunks - 1))),
            pl.BlockSpec(memory_space=pl.ANY),
        ],
        out_specs=(pl.BlockSpec((chips, rows, share), lambda i: (0, 0, 0)),) * 2,
        scratch_shapes=[
            pltpu.VMEM((slots, 2, 2, rows // 2, width), jnp.float32),
            pltpu.VMEM((chunks, 2, 2, rows // 2, width), bf16),
            pltpu.VMEM((chunks, 2, 2, rows // 2, width), bf16),
            pltpu.VMEM((chunks, 2, rows // 2, width), bf16),
            pltpu.VMEM((wide, rows, share), jnp.float32),
            pltpu.VMEM((chunks, width, depth), bf16),
            dma((chunks, 2)),
            dma((chunks, 2)),
            dma((chunks, 2)),
            dma((chunks, 2)),
            dma((chunks,)),
        ],
        compiler_params=pltpu.CompilerParams(
            collective_id=1, has_side_effects=True, vmem_limit_bytes=VMEM_LIMIT
        ),
        name="ffn",
    )(piece, gate_weight, up_weight, down_weight)

    steps = chips.bit_length() - 1
    ffn_out = pl.pallas_call(
        functools.partial(scatter_kernel, wide, narrow),
        out_shape=jax.ShapeDtypeStruct((batch_rows, model), bf16),
        in_specs=[vmem, vmem],
        out_specs=vmem,
        scratch_shapes=[
            pltpu.VMEM((chips, rows, share), bf16),
            pltpu.VMEM((chips, rows, share), jnp.float32),
            pltpu.VMEM((chips, rows, share), bf16),
            pltpu.VMEM((steps, chips, rows, share), bf16),
            pltpu.VMEM((rows, share), jnp.float32),
            pltpu.VMEM((devices, batch_rows, share), bf16),
            pltpu.VMEM((devices, batch_rows, share), bf16),
            dma((chips,)),
            dma((chips,)),
            dma((2, chips)),
            dma((2, chips)),
            dma((devices,)),
            dma((devices,)),
        ],
        compiler_params=pltpu.CompilerParams(
            collective_id=2, has_side_effects=True, vmem_limit_bytes=VMEM_LIMIT
        ),
        name="scatter",
    )(keep, give)
    return (attended, ffn_out)


def solution(mesh):
    in_specs = (
        P(("wide", "narrow"), None),
        P(("wide", "narrow"), None),
        P(("wide", "narrow"), None, None, None),
        P(("wide", "narrow"), None, None, None),
        P(("wide", "narrow")),
        P(("wide", "narrow")),
        P(),
        P(),
        P("narrow", "wide"),
        P("narrow", "wide"),
        P("wide", "narrow"),
    )
    out_specs = (P(("wide", "narrow"), None), P(("wide", "narrow"), None))
    return jax.shard_map(
        functools.partial(per_device, mesh.shape["wide"], mesh.shape["narrow"]),
        mesh=mesh,
        in_specs=in_specs,
        out_specs=out_specs,
        check_vma=False,
    )
```
